32 devices in a mesh: dp: 8 (over z, x), tp: 4 (over y, core).
Axes of the slice: x: 2, y: 2, z: 4, core: 2. Of those that a mesh axis runs over, the one named last changes fastest.
Arguments:
- layer_input: bfloat16 [8, 1024, 768], P('dp', 'tp'), may hold values from -6 to 6
- lengths: int32 [8], P('dp'), may hold values from 8 to 1024, as said below
- w_qkv: bfloat16 [768, 3, 768], P(None, None, 'tp'), may hold values from -0.21875 to 0.21875
- w_out: bfloat16 [768, 768], P('tp'), may hold values from -1.75 to 1.75
- w_gate: bfloat16 [768, 3072], P(None, 'tp'), may hold values from -0.21875 to 0.21875
- w_up: bfloat16 [768, 3072], P(None, 'tp'), may hold values from -0.21875 to 0.21875
- w_down: bfloat16 [3072, 768], P('tp'), may hold values from -0.109375 to 0.109375
- gain_one: float32 [768], replicated, may hold values from 0.5 to 1.5
- bias_one: float32 [768], replicated, may hold values from -1.8 to 1.8
- gain_two: float32 [768], replicated, may hold values from 0.5 to 1.5
- bias_two: float32 [768], replicated, may hold values from -1.8 to 1.8
- cotangent: bfloat16 [8, 1024, 768], P('dp', 'tp'), may hold values from -6 to 6
Outputs:
- output: bfloat16 [8, 1024, 768], P('dp', 'tp')
- input_grad: float32 [8, 1024, 768], P('dp', 'tp')
- qkv_grad: float32 [768, 3, 768], P('dp', None, 'tp')
- out_grad: float32 [768, 768], P('tp', 'dp')
- gate_grad: float32 [768, 3072], P('dp', 'tp')
- up_grad: float32 [768, 3072], P('dp', 'tp')
- down_grad: float32 [3072, 768], P('tp', 'dp')
- gain_one_grad: float32 [768], replicated
- bias_one_grad: float32 [768], replicated
- gain_two_grad: float32 [768], replicated
- bias_two_grad: float32 [768], replicated
The draws below stay inside these ranges and needn't reach their ends.
Inputs may be any that keep to these rules, and one draw needn't show every extreme that they name: `lengths`: each row's count of real tokens; later positions of the row are padding. Some row has exactly 1024 and some row exactly 8.
All inputs are finite; a program needn't handle non-finite values.
Results may differ from the reference program's by a relative error of at most 0.017.
Values may be sent and summed in bfloat16 or wider, within the bound.
No kernel may reach another device: no remote copies, remote signals or barrier semaphores. Data moves between devices by JAX's collectives and lax.ppermute only.
A program may use at most 128 MiB of HBM per device.

```python
import math
import jax
import jax.numpy as jnp
from jax import lax

D = 768
H = 12
HD = 64
FF = 3072
SEQ = 1024
BATCH = 8


def draw_lengths(key, part):
    key_query, key_document, key_choose = jax.random.split(key, 3)
    query_len = jax.random.randint(key_query, (BATCH,), 8, min(64, SEQ) + 1)
    document_len = jax.random.randint(key_document, (BATCH,), max(8, SEQ // 4), SEQ + 1)
    chooser = jax.random.randint(key_choose, (BATCH,), 0, 3)
    lengths = jnp.where(chooser == 0, query_len, document_len)
    lengths = lengths.at[0].set(SEQ).at[1].set(8)
    return lengths.astype(jnp.int32)


def strengthened(array, stream_key, source, target, parts, factor):
    owner, partner = [(jnp.arange(array.shape[dim]) // (array.shape[dim] // parts)).reshape([-1 if axis == dim else 1 for axis in range(array.ndim)]) for dim in (source, target)]
    chosen = jax.random.permutation(stream_key, parts)[partner]
    strong = (owner == chosen) | (owner == (partner + parts // 2) % parts)
    return jnp.where(strong, factor * array, array)


def levels(rng, extent, pieces, least, top_value):
    level = 1.0
    for axis_at, parts in pieces:
        heights = jax.random.uniform(jax.random.fold_in(jax.random.fold_in(rng, 6), axis_at), (parts,), jnp.float32, least / len(pieces), top_value / len(pieces))
        level = level * jnp.repeat(jnp.exp(heights), extent[axis_at] // parts).reshape((-1,) + (1,) * (len(extent) - 1 - axis_at))
    return level


def scatter_about(rng, dims, deviation, bound, pieces=(), kind=jnp.bfloat16):
    entries = deviation * jax.random.normal(rng, dims, jnp.float32)
    if pieces:
        entries = entries * levels(rng, dims, pieces, -0.22, 0.18)
    return jnp.clip(entries, -bound, bound).astype(kind)


def bell_draw_with(key, extent, width, reach, shards, heavy, held_as=jnp.bfloat16):
    array = width * jax.random.normal(key, extent, jnp.float32)
    if shards:
        array = array * levels(key, extent, shards, -0.22, 0.18)
    return jnp.clip(strengthened(array, jax.random.fold_in(key, 3), *heavy), -reach, reach).astype(held_as)


def setup_inputs(seed: int = 0) -> dict:
    arg_keys = jax.random.split(jax.random.key(seed), 13)
    layer_input = scatter_about(arg_keys[0], (BATCH, SEQ, D), 1.0, 6.0, ((0, 8), (1, 4)))
    lengths = draw_lengths(jax.random.fold_in(arg_keys[12], 71), 0)
    w_qkv = scatter_about(arg_keys[2], (D, 3, D), D ** -0.5, 0.21875, ((2, 4),))
    w_out = scatter_about(arg_keys[3], (D, D), (D // 64) ** -0.5, 1.75, ((0, 4),))
    w_gate = scatter_about(arg_keys[4], (D, FF), D ** -0.5, 0.21875, ((1, 4),))
    w_up = scatter_about(arg_keys[5], (D, FF), D ** -0.5, 0.21875, ((1, 4),))
    w_down = scatter_about(arg_keys[6], (FF, D), FF ** -0.5, 0.109375, ((0, 4),))
    gain_one = jnp.clip(1.0 + 0.1 * jax.random.normal(arg_keys[7], (D,), jnp.float32), 0.5, 1.5)
    bias_one = scatter_about(arg_keys[8], (D,), 0.3, 1.8, (), jnp.float32)
    gain_two = jnp.clip(1.0 + 0.1 * jax.random.normal(arg_keys[9], (D,), jnp.float32), 0.5, 1.5)
    bias_two = scatter_about(arg_keys[10], (D,), 0.3, 1.8, (), jnp.float32)
    cotangent = bell_draw_with(arg_keys[11], (BATCH, SEQ, D), 1.0, 6.0, ((0, 8), (1, 4)), (0, 2, 8, 2.0))
    return dict(layer_input=layer_input, lengths=lengths, w_qkv=w_qkv, w_out=w_out, w_gate=w_gate, w_up=w_up, w_down=w_down, gain_one=gain_one, bias_one=bias_one, gain_two=gain_two, bias_two=bias_two, cotangent=cotangent)


@jax.custom_vjp
def low(v):
    return lax.optimization_barrier(v.astype(jnp.bfloat16)).astype(jnp.float32)

@jax.custom_vjp
def low_back(v):
    return v

def low_keep(v):
    return (low(v), None)

def low_pass(kept, grad):
    return (grad,)

def back_keep(v):
    return (v, None)

def back_low(kept, grad):
    return (low(grad),)
low.defvjp(low_keep, low_pass)
low_back.defvjp(back_keep, back_low)
highest = lax.Precision.HIGHEST
masked_score = -1e+30
epsilon = 1e-05

def angle_tables(positions_count, head_width):
    position = jnp.arange(positions_count, dtype=jnp.float32)
    frequency = 1000.0 ** (-jnp.arange(head_width // 2, dtype=jnp.float32) * 2.0 / head_width)
    angles = position[:, None] * frequency[None, :]
    return (jnp.cos(angles)[:, None, :], jnp.sin(angles)[:, None, :])

def rotate(values, cosine, sine_table, direction):
    half_width = values.shape[-1] // 2
    lower = values[..., :half_width]
    upper = values[..., half_width:]
    return jnp.concatenate([lower * cosine - direction * upper * sine_table, upper * cosine + direction * lower * sine_table], axis=-1)

def layer_norm(values, gain_vec, bias_vec):
    center = values - lax.optimization_barrier(jnp.mean(values, axis=-1, keepdims=True))
    spread = lax.optimization_barrier(jnp.mean(center * center, axis=-1, keepdims=True))
    return center * lax.rsqrt(spread + epsilon) * gain_vec + bias_vec

def forward_rows(inputs, mask_rows, params):
    w_qkv, w_out, w_gate, w_up, w_down, gain_one, bias_one, gain_two, bias_two = params
    group_size = inputs.shape[0]
    seq_len = inputs.shape[1]
    cosine, sine_table = angle_tables(seq_len, HD)
    projected = low_back(jnp.einsum('gsd,dce->gsce', inputs, w_qkv, precision=highest))
    projected = projected.reshape(group_size, seq_len, 3, H, HD)
    queries = low(rotate(projected[:, :, 0], cosine, sine_table, 1.0))
    keys_rot = low(rotate(projected[:, :, 1], cosine, sine_table, 1.0))
    values_low = low(projected[:, :, 2])
    scores = low_back(jnp.einsum('gshe,gthe->ghst', queries, keys_rot, precision=highest) * HD ** (-0.5))
    scores = jnp.where(mask_rows[:, None, None, :] > 0.5, scores, masked_score)
    row_max = lax.optimization_barrier(jnp.max(scores, axis=-1, keepdims=True))
    exps_raw = jnp.exp(scores - row_max)
    attn_probs = low(exps_raw / lax.optimization_barrier(jnp.sum(exps_raw, axis=-1, keepdims=True)))
    heads_out = jnp.einsum('ghst,gthe->gshe', attn_probs, values_low, precision=highest)
    heads_out = low_back(low(heads_out)).reshape(group_size, seq_len, H * HD)
    attn_out = low_back(jnp.einsum('gsk,kd->gsd', heads_out, w_out, precision=highest))
    first_norm = layer_norm(inputs + attn_out, gain_one, bias_one)
    first_low = low(first_norm)
    gate_act = low_back(jnp.einsum('gsd,df->gsf', first_low, w_gate, precision=highest))
    up_act = low_back(jnp.einsum('gsd,df->gsf', first_low, w_up, precision=highest))
    hidden = low(gate_act * jax.nn.sigmoid(gate_act) * up_act)
    ffn_out = low_back(jnp.einsum('gsf,fd->gsd', hidden, w_down, precision=highest))
    return layer_norm(first_norm + ffn_out, gain_two, bias_two) * mask_rows[:, :, None]

def reference(layer_input, lengths, w_qkv, w_out, w_gate, w_up, w_down, gain_one, bias_one, gain_two, bias_two, cotangent):
    group_size = math.gcd(BATCH, 2)
    mask_all = (jnp.arange(SEQ, dtype=jnp.int32)[None, :] < lengths[:, None].astype(jnp.int32)).astype(jnp.float32)
    params = tuple((weight_item.astype(jnp.float32) for weight_item in (w_qkv, w_out, w_gate, w_up, w_down, gain_one, bias_one, gain_two, bias_two)))

    def whole_batch(inputs, weights_all):
        row_blocks = inputs.reshape(BATCH // group_size, group_size, SEQ, D)
        mask_blocks = mask_all.reshape(BATCH // group_size, group_size, SEQ)

        def one_group(operands):
            return forward_rows(operands[0], operands[1], weights_all)
        outputs = lax.map(jax.checkpoint(one_group), (row_blocks, mask_blocks))
        return outputs.reshape(BATCH, SEQ, D)
    result, pullback = jax.vjp(whole_batch, layer_input.astype(jnp.float32), params)
    input_grad, param_grads = pullback(cotangent.astype(jnp.float32))
    return (result.astype(jnp.bfloat16), input_grad, param_grads[0], param_grads[1], param_grads[2], param_grads[3], param_grads[4], param_grads[5], param_grads[6], param_grads[7], param_grads[8])
```

```python
import jax
import jax.numpy as jnp
from jax import lax
from jax.sharding import PartitionSpec as P

HD = 64
CHUNKS = 2

masked_score = -1e30
epsilon = 1e-05


BF = jnp.bfloat16
F32 = jnp.float32


def swap(values, axis, mask):
    size = lax.axis_size(axis)
    return lax.ppermute(values, axis, [(i, i ^ mask) for i in range(size)])


def gather_blocks(block):
    across = swap(block, "tp", 2)
    beside = swap(block, "tp", 1)
    return [block, beside, across, swap(across, "tp", 1)]


def scatter_blocks(blocks):
    rows = blocks[0].shape[0]
    sent = jnp.concatenate([blocks[1], blocks[3]], 0).astype(BF)
    got = swap(sent, "tp", 1).astype(F32)
    away = (blocks[2] + got[rows:]).astype(BF)
    back = swap(away, "tp", 2)
    return blocks[0] + got[:rows] + back.astype(F32)


def scatter_dp(grad):
    size = lax.axis_size("dp")
    me = lax.axis_index("dp")
    cols = grad.shape[1]
    rows = grad.shape[0] // size
    step = 1
    while step < size:
        bit = (me // step) % 2
        left = size // step
        view = grad.reshape(left // 2, 2, rows, cols)
        send = lax.dynamic_index_in_dim(view, 1 - bit, 1, keepdims=False).astype(BF)
        keep = lax.dynamic_index_in_dim(view, bit, 1, keepdims=False)
        grad = keep.astype(F32) + swap(send, "dp", step).astype(F32)
        step *= 2
        if step < size:
            grad = grad.astype(BF)
    return grad.reshape(rows, cols)


def sum_all(values):
    for axis in ("tp", "dp"):
        step = 1
        while step < lax.axis_size(axis):
            values = values + swap(values, axis, step)
            step *= 2
    return values


def rotate(values, cosine, sine_table, direction):
    half_width = values.shape[-1] // 2
    lower = values[..., :half_width]
    upper = values[..., half_width:]
    return jnp.concatenate(
        [
            lower * cosine - direction * upper * sine_table,
            upper * cosine + direction * lower * sine_table,
        ],
        axis=-1,
    )


def norm_core(values):
    center = values - jnp.mean(values, axis=-1, keepdims=True)
    inverse = lax.rsqrt(jnp.mean(center * center, axis=-1, keepdims=True) + epsilon)
    return center * inverse, inverse


def norm_backward(upstream, normed, inverse, gain_vec):
    scaled = upstream * gain_vec
    return inverse * (
        scaled
        - jnp.mean(scaled, axis=-1, keepdims=True)
        - normed * jnp.mean(scaled * normed, axis=-1, keepdims=True)
    )


def dot(a, b, dims):
    return lax.dot_general(a, b, (dims, ((), ())), preferred_element_type=F32)


def body(
    layer_input,
    lengths,
    w_qkv,
    w_out,
    w_gate,
    w_up,
    w_down,
    gain_one,
    bias_one,
    gain_two,
    bias_two,
    cotangent,
):
    _, piece, width = layer_input.shape
    local_width = w_qkv.shape[2]
    heads = local_width // HD
    tp = lax.axis_size("tp")
    seq = piece * tp
    me = lax.axis_index("tp")
    scale = HD ** (-0.5)
    length = lengths[0]
    own = layer_input[0]
    cot = cotangent[0]
    wq = w_qkv.reshape(width, 3 * local_width)
    part = piece // CHUNKS

    gathered = jnp.concatenate(gather_blocks(own), 0)

    block_of = jnp.bitwise_xor(me, jnp.arange(tp, dtype=jnp.int32))
    positions = (block_of[:, None] * piece + jnp.arange(piece, dtype=jnp.int32)[None]).reshape(seq)
    frequency = 1000.0 ** (-jnp.arange(HD // 2, dtype=F32) * 2.0 / HD)
    angles = positions.astype(F32)[:, None] * frequency[None, :]
    cosine, sine_table = jnp.cos(angles)[:, None, :], jnp.sin(angles)[:, None, :]
    key_valid = positions < length
    row_valid = (me * piece + jnp.arange(piece, dtype=jnp.int32) < length).astype(F32)[:, None]

    projected = dot(gathered, wq, ((1,), (0,))).reshape(seq, 3, heads, HD)
    queries = rotate(projected[:, 0], cosine, sine_table, 1.0).astype(BF)
    keys_rot = rotate(projected[:, 1], cosine, sine_table, 1.0).astype(BF)
    values_low = projected[:, 2].astype(BF)

    def rows_of(array, c):
        view = array.reshape((tp, CHUNKS, part) + array.shape[1:])
        return view[:, c].reshape((tp * part,) + array.shape[1:])

    def split4(array):
        return [array[j * part : (j + 1) * part] for j in range(tp)]

    def piece_of(array, c):
        return array[c * part : (c + 1) * part]

    firsts = []
    heads_kept, totals = [], []
    for c in range(CHUNKS):
        query = rows_of(queries, c)
        scores = (
            jnp.einsum("she,the->hst", query, keys_rot, preferred_element_type=F32) * scale
        )
        scores = jnp.where(key_valid[None, None, :], scores, masked_score)
        row_max = jnp.max(scores, axis=-1, keepdims=True)
        exps = jnp.exp(scores - row_max)
        total = jnp.sum(exps, axis=-1, keepdims=True)
        probs = (exps / total).astype(BF)
        mixed = jnp.einsum("hst,the->she", probs, values_low, preferred_element_type=F32)
        mixed = mixed.astype(BF).reshape(tp * part, local_width)
        heads_kept.append(mixed)
        totals.append(row_max + jnp.log(total))
        attn = scatter_blocks(split4(dot(mixed, w_out, ((1,), (0,)))))
        n1, r1 = norm_core(piece_of(own, c).astype(F32) + attn)
        first = n1 * gain_one + bias_one
        firsts.append((n1, r1, first))

    saved = []
    for c in range(CHUNKS):
        n1, r1, first = firsts[c]
        ffn_input = jnp.concatenate(gather_blocks(first.astype(BF)), 0)
        gate = dot(ffn_input, w_gate, ((1,), (0,)))
        up = dot(ffn_input, w_up, ((1,), (0,)))
        sg = jax.nn.sigmoid(gate)
        hidden = (gate * sg * up).astype(BF)
        ffn = scatter_blocks(split4(dot(hidden, w_down, ((1,), (0,)))))
        saved.append((ffn_input, gate, up, sg, hidden, ffn))

    outputs, seconds = [], []
    small = jnp.zeros((4, width), F32)
    for c in range(CHUNKS):
        n1, r1, first = firsts[c]
        ffn = saved[c][5]
        valid = piece_of(row_valid, c)
        n2, r2 = norm_core(first + ffn)
        outputs.append((valid * (n2 * gain_two + bias_two)).astype(BF))
        g_out = piece_of(cot, c).astype(F32) * valid
        g_second = norm_backward(g_out, n2, r2, gain_two)
        small = small.at[2].add(jnp.sum(g_out * n2, 0)).at[3].add(jnp.sum(g_out, 0))
        seconds.append((g_second, jnp.concatenate(gather_blocks(g_second.astype(BF)), 0)))

    residuals = []
    down_grad = gate_grad = up_grad = 0.0
    for c in range(CHUNKS):
        n1, r1, first = firsts[c]
        ffn_input, gate, up, sg, hidden, _ = saved[c]
        g_second, g_ffn = seconds[c]
        g_hidden = dot(g_ffn, w_down, ((1,), (1,)))
        g_gate = (g_hidden * up * sg * (1.0 + gate * (1.0 - sg))).astype(BF)
        g_up = (g_hidden * gate * sg).astype(BF)
        inner = dot(g_gate, w_gate, ((1,), (1,))) + dot(g_up, w_up, ((1,), (1,)))
        g_first = g_second + scatter_blocks(split4(inner))
        g_res = norm_backward(g_first, n1, r1, gain_one)
        small = small.at[0].add(jnp.sum(g_first * n1, 0)).at[1].add(jnp.sum(g_first, 0))
        residuals.append((g_res, jnp.concatenate(gather_blocks(g_res.astype(BF)), 0)))
        down_grad = down_grad + dot(g_ffn, hidden, ((0,), (0,)))
        gate_grad = gate_grad + dot(ffn_input, g_gate, ((0,), (0,)))
        up_grad = up_grad + dot(ffn_input, g_up, ((0,), (0,)))
    down_grad = scatter_dp(down_grad.astype(BF)).T
    gate_grad = scatter_dp(gate_grad.astype(BF))
    up_grad = scatter_dp(up_grad.astype(BF))

    out_grad = 0.0
    g_query, g_keys, g_values = [], 0.0, 0.0
    for c in range(CHUNKS):
        g_attn = residuals[c][1]
        mixed = heads_kept[c]
        out_grad = out_grad + dot(g_attn, mixed, ((0,), (0,)))
        g_heads = dot(g_attn, w_out, ((1,), (1,))).astype(BF).reshape(tp * part, heads, HD)
        query = rows_of(queries, c)
        scores = (
            jnp.einsum("she,the->hst", query, keys_rot, preferred_element_type=F32) * scale
        )
        scores = jnp.where(key_valid[None, None, :], scores, masked_score)
        f = jnp.exp(scores - totals[c])
        g_p = jnp.einsum("she,the->hst", g_heads, values_low, preferred_element_type=F32)
        delta = jnp.sum(f * g_p, axis=-1, keepdims=True)
        g_scores = (f * (g_p - delta)).astype(BF)
        g_query.append(
            jnp.einsum("hst,the->she", g_scores, keys_rot, preferred_element_type=F32) * scale
        )
        g_keys = g_keys + (
            jnp.einsum("hst,she->the", g_scores, query, preferred_element_type=F32) * scale
        )
        g_values = g_values + jnp.einsum(
            "hst,she->the", f.astype(BF), g_heads, preferred_element_type=F32
        )
    out_grad = scatter_dp(out_grad.astype(BF)).T
    g_query = jnp.stack([g.reshape(tp, part, heads, HD) for g in g_query], 1)
    g_query = g_query.reshape(seq, heads, HD)
    g_qkv = jnp.stack(
        [
            rotate(g_query, cosine, sine_table, -1.0),
            rotate(g_keys, cosine, sine_table, -1.0),
            g_values,
        ],
        axis=1,
    )
    g_qkv = g_qkv.reshape(seq, 3 * local_width).astype(BF)
    qkv_grad = scatter_dp(dot(gathered, g_qkv, ((0,), (0,))).astype(BF))
    input_parts = dot(g_qkv, wq, ((1,), (1,)))
    input_parts = [input_parts[j * piece : (j + 1) * piece] for j in range(tp)]
    g_res = jnp.concatenate([r[0] for r in residuals], 0)
    input_grad = g_res + scatter_blocks(input_parts)
    small = sum_all(small)
    return (
        jnp.concatenate(outputs, 0)[None],
        input_grad[None],
        qkv_grad.reshape(-1, 3, local_width),
        out_grad,
        gate_grad,
        up_grad,
        down_grad,
        small[0],
        small[1],
        small[2],
        small[3],
    )


def solution(mesh):
    placed = (
        P("dp", "tp", None),
        P("dp"),
        P(None, None, "tp"),
        P("tp", None),
        P(None, "tp"),
        P(None, "tp"),
        P("tp", None),
        P(),
        P(),
        P(),
        P(),
        P("dp", "tp", None),
    )
    return jax.shard_map(
        body,
        mesh=mesh,
        in_specs=placed,
        out_specs=(
            P("dp", "tp", None),
            P("dp", "tp", None),
            P("dp", None, "tp"),
            P("tp", "dp"),
            P("dp", "tp"),
            P("dp", "tp"),
            P("tp", "dp"),
            P(),
            P(),
            P(),
            P(),
        ),
        check_vma=False,
    )
```

```python
import functools

import jax
import jax.numpy as jnp
from jax import lax
from jax.experimental import pallas as pl
from jax.experimental.pallas import tpu as pltpu
from jax.sharding import PartitionSpec as P

HD = 64
CHUNKS = 2
TP = 4

masked_score = -1e30
epsilon = 1e-05


BF = jnp.bfloat16
F32 = jnp.float32
NN = ((1,), (0,))
NT = ((1,), (1,))
TN = ((0,), (0,))


def dot(a, b, dims):
    return lax.dot_general(a, b, (dims, ((), ())), preferred_element_type=F32)


def swap(values, axis, mask):
    size = lax.axis_size(axis)
    return lax.ppermute(values, axis, [(i, i ^ mask) for i in range(size)])


def gather_blocks(block):
    across = swap(block, "tp", 2)
    beside = swap(block, "tp", 1)
    return [block, beside, across, swap(across, "tp", 1)]


def scatter_blocks(send, keep_away):
    rows = send.shape[0] // 2
    got = swap(send, "tp", 1)
    away = (keep_away + got[rows:].astype(F32)).astype(BF)
    return got, swap(away, "tp", 2)


def scatter_dp(grad):
    size = lax.axis_size("dp")
    me = lax.axis_index("dp")
    cols = grad.shape[1]
    rows = grad.shape[0] // size
    step = 1
    while step < size:
        bit = (me // step) % 2
        left = size // step
        view = grad.reshape(left // 2, 2, rows, cols)
        send = lax.dynamic_index_in_dim(view, 1 - bit, 1, keepdims=False).astype(BF)
        keep = lax.dynamic_index_in_dim(view, bit, 1, keepdims=False)
        grad = keep.astype(F32) + swap(send, "dp", step).astype(F32)
        step *= 2
        if step < size:
            grad = grad.astype(BF)
    return grad.reshape(rows, cols)


def sum_all(values):
    for axis in ("tp", "dp"):
        step = 1
        while step < lax.axis_size(axis):
            values = values + swap(values, axis, step)
            step *= 2
    return values


def call(kernel, name, outs, args, flops, scratch=(), smem=0):
    specs = [pl.BlockSpec(memory_space=pltpu.SMEM)] * smem
    specs += [pl.BlockSpec(memory_space=pltpu.VMEM)] * (len(args) - smem)
    shapes = [jax.ShapeDtypeStruct(s, d) for s, d in outs]
    moved = sum(a.size * a.dtype.itemsize for a in args)
    moved += sum(s.size * s.dtype.itemsize for s in shapes)
    return pl.pallas_call(
        kernel,
        name=name,
        out_shape=shapes,
        in_specs=specs,
        out_specs=[pl.BlockSpec(memory_space=pltpu.VMEM)] * len(shapes),
        scratch_shapes=list(scratch),
        compiler_params=pltpu.CompilerParams(vmem_limit_bytes=40 * 1024 * 1024),
        cost_estimate=pl.CostEstimate(flops=flops, bytes_accessed=moved, transcendentals=0),
    )(*args)


def turn(values, cosine, sine, direction):
    half = values.shape[0] // 2
    lower, upper = values[:half], values[half:]
    if direction > 0:
        return jnp.concatenate([lower * cosine - upper * sine, upper * cosine + lower * sine], 0)
    return jnp.concatenate([lower * cosine + upper * sine, upper * cosine - lower * sine], 0)


def three_parts(row):
    hi = row.astype(BF).astype(F32)
    rest = row - hi
    mid = rest.astype(BF).astype(F32)
    return hi, mid, rest - mid


def extra_rows(first, parts, count):
    row = lax.broadcasted_iota(jnp.int32, (64, count), 0)
    out = jnp.where(row == 0, first, 0.0)
    for k, part in enumerate(parts):
        out = jnp.where(row == k + 1, part, out)
    return out


def qkv_kernel(info, b0, b1, b2, b3, wt, cos, sin, pos, xg, qt, q, kt, k, vt, v, full):
    blocks = (b0, b1, b2, b3)
    piece = b0.shape[0]
    part = piece // CHUNKS
    heads = wt.shape[0] // (3 * HD)
    for j in range(TP):
        for c in range(CHUNKS):
            at = (c * TP + j) * part
            xg[at : at + part, :] = blocks[j][c * part : (c + 1) * part, :]
    seq = piece * TP
    half = seq // CHUNKS
    for c in range(CHUNKS):
        cols = slice(c * half, (c + 1) * half)
        full[:, cols] = dot(wt[...], xg[cols, :], NT)
    ones = (1.0, 1.0, 1.0)
    bias = jnp.where(pos[...] < info[0], 0.0, masked_score)
    for c in range(CHUNKS):
        cols = slice(c * half, (c + 1) * half)
        cosine, sine = cos[:, cols], sin[:, cols]
        for h in range(heads):
            at = h * HD
            query = turn(full[at : at + HD, cols], cosine, sine, 1) * HD**-0.5
            query = jnp.concatenate([query, extra_rows(1.0, (0.0, 0.0, 0.0), half)], 0)
            qt[h, :, cols] = query.astype(BF)
            q[h, cols, :] = query.T.astype(BF)
            at = (heads + h) * HD
            keys = turn(full[at : at + HD, cols], cosine, sine, 1)
            keys = jnp.concatenate([keys, extra_rows(bias[:, cols], ones, half)], 0)
            kt[h, :, cols] = keys[:HD].astype(BF)
            k[h, cols, :] = keys.T.astype(BF)
            at = (2 * heads + h) * HD
            values = jnp.concatenate([full[at : at + HD, cols], extra_rows(0.0, ones, half)], 0)
            vt[h, :, cols] = values.astype(BF)
            v[h, cols, :] = values.T.astype(BF)


def attend_kernel(chunk, qt, k, vt, wo, send, keep0, keep2, headst, lse):
    heads = qt.shape[0]
    count = headst.shape[1]
    part = count // TP
    tile = 256
    tiles = count // tile

    def step(i, _):
        h, at = i // tiles, pl.multiple_of((i % tiles) * tile, tile)
        query = qt[h, :, pl.ds(chunk * count + at, tile)]
        scores = dot(k[h], query, NN)
        top = jnp.max(scores, axis=0, keepdims=True)
        exps = jnp.exp(scores - top).astype(BF)
        mixed = dot(vt[h, :80, :], exps, NN)
        total = mixed[HD + 1 : HD + 2]
        mixed = (mixed[:HD] / total).astype(BF)
        headst[pl.ds(pl.multiple_of(h * HD, HD), HD), pl.ds(at, tile)] = mixed
        lse[h, :, pl.ds(at, tile)] = top + jnp.log(total)
        return 0

    lax.fori_loop(0, heads * tiles, step, 0)
    mixed = headst[...].T
    out = dot(mixed, wo[...], NN)
    keep0[...] = out[:part]
    send[:part, :] = out[part : 2 * part].astype(BF)
    keep2[...] = out[2 * part : 3 * part]
    send[part:, :] = out[3 * part :].astype(BF)


def norm(values):
    center = values - jnp.mean(values, axis=-1, keepdims=True)
    inverse = lax.rsqrt(jnp.mean(center * center, axis=-1, keepdims=True) + epsilon)
    return center * inverse, inverse


def norm_grad(upstream, normed, inverse, gain):
    scaled = upstream * gain
    return inverse * (
        scaled
        - jnp.mean(scaled, axis=-1, keepdims=True)
        - normed * jnp.mean(scaled * normed, axis=-1, keepdims=True)
    )


def first_kernel(x, keep0, got, back, gain, bias, n1, r1, low):
    part = x.shape[0]
    summed = x[...].astype(F32) + keep0[...] + got[:part].astype(F32) + back[...].astype(F32)
    normed, inverse = norm(summed)
    n1[...] = normed
    r1[...] = inverse
    low[...] = (normed * gain[...] + bias[...]).astype(BF)


def ffn_kernel(b0, b1, b2, b3, wg, wu, wd, x, hidden, da, db, send, keep0, keep2):
    part, width = b0.shape
    for j, block in enumerate((b0, b1, b2, b3)):
        x[j * part : (j + 1) * part, :] = block[...]
    tile = 256
    for n in range(wg.shape[1] // tile):
        cols = slice(n * tile, (n + 1) * tile)
        gate = dot(x[...], wg[:, cols], NN)
        up = dot(x[...], wu[:, cols], NN)
        sg = jax.nn.sigmoid(gate)
        act = gate * sg
        hidden[:, cols] = (act * up).astype(BF)
        da[:, cols] = (up * sg * (1.0 + gate * (1.0 - sg))).astype(BF)
        db[:, cols] = act.astype(BF)
    for n in range(width // tile):
        cols = slice(n * tile, (n + 1) * tile)
        out = dot(hidden[...], wd[:, cols], NN)
        keep0[:, cols] = out[:part]
        send[:part, cols] = out[part : 2 * part].astype(BF)
        keep2[:, cols] = out[2 * part : 3 * part]
        send[part:, cols] = out[3 * part :].astype(BF)


def second_kernel(
    chunk, info, n1, gain_one, bias_one, keep0, got, back, gain, bias, cot, out, gsec, glow, small
):
    part = n1.shape[0]
    first = n1[...] * gain_one[...] + bias_one[...]
    ffn = keep0[...] + got[:part].astype(F32) + back[...].astype(F32)
    n2, r2 = norm(first + ffn)
    row = info[1] + chunk * part + lax.broadcasted_iota(jnp.int32, (part, 1), 0)
    valid = jnp.where(row < info[0], 1.0, 0.0)
    out[...] = (valid * (n2 * gain[...] + bias[...])).astype(BF)
    g_out = cot[...].astype(F32) * valid
    g_second = norm_grad(g_out, n2, r2, gain[...])
    gsec[...] = g_second
    glow[...] = g_second.astype(BF)
    small[0:1, :] = jnp.sum(g_out * n2, axis=0, keepdims=True)
    small[1:2, :] = jnp.sum(g_out, axis=0, keepdims=True)


def ffn_back_kernel(b0, b1, b2, b3, wg, wu, wd, da, db, gf, gg, send, keep0, keep2):
    part, width = b0.shape
    for j, block in enumerate((b0, b1, b2, b3)):
        gf[j * part : (j + 1) * part, :] = block[...]
    tile = 256
    hidden = wg.shape[1]
    for n in range(hidden // tile):
        cols = slice(n * tile, (n + 1) * tile)
        more = slice(hidden + n * tile, hidden + (n + 1) * tile)
        g_hidden = dot(gf[...], wd[cols, :], NT)
        gg[:, cols] = (g_hidden * da[:, cols].astype(F32)).astype(BF)
        gg[:, more] = (g_hidden * db[:, cols].astype(F32)).astype(BF)
    for n in range(width // tile):
        cols = slice(n * tile, (n + 1) * tile)
        out = dot(gg[:, :hidden], wg[cols, :], NT) + dot(gg[:, hidden:], wu[cols, :], NT)
        keep0[:, cols] = out[:part]
        send[:part, cols] = out[part : 2 * part].astype(BF)
        keep2[:, cols] = out[2 * part : 3 * part]
        send[part:, cols] = out[3 * part :].astype(BF)


def first_back_kernel(gsec, keep0, got, back, n1, r1, gain, gres, low, small):
    part = n1.shape[0]
    g_first = gsec[...] + keep0[...] + got[:part].astype(F32) + back[...].astype(F32)
    normed = n1[...]
    g_res = norm_grad(g_first, normed, r1[...], gain[...])
    gres[...] = g_res
    low[...] = g_res.astype(BF)
    small[0:1, :] = jnp.sum(g_first * normed, axis=0, keepdims=True)
    small[1:2, :] = jnp.sum(g_first, axis=0, keepdims=True)


def attend_back_kernel(*refs):
    blocks = refs[: TP * CHUNKS]
    wo, qt, q, kt, k, v, cos, sin = refs[TP * CHUNKS : TP * CHUNKS + 8]
    rest = refs[TP * CHUNKS + 8 :]
    headst, lse = rest[:CHUNKS], rest[CHUNKS : 2 * CHUNKS]
    ga, gqkv, gt, g, dk, dv = rest[2 * CHUNKS :]
    heads = qt.shape[0]
    seq = ga.shape[0]
    half = seq // CHUNKS
    part = half // TP
    tile = 256
    for b, block in enumerate(blocks):
        ga[b * part : (b + 1) * part, :] = block[...]
    for c in range(CHUNKS):
        rows = slice(c * half, (c + 1) * half)
        gt[:, rows] = dot(wo[...], ga[rows, :], NT).astype(BF)
        for h in range(heads):
            g[h, rows, :] = dot(ga[rows, :], wo[h * HD : (h + 1) * HD, :], NT).astype(BF)

    def one_head(h, _):
        at_head = pl.multiple_of(h * HD, HD)
        for c in range(CHUNKS):
            for n in range(half // tile):
                at = slice(n * tile, (n + 1) * tile)
                cols = slice(c * half + n * tile, c * half + (n + 1) * tile)
                total = lse[c][h, :, at]
                query = jnp.concatenate(
                    [
                        qt[h, :HD, cols],
                        extra_rows(1.0, three_parts(-total), tile).astype(BF),
                    ],
                    0,
                )
                grad = gt[pl.ds(at_head, HD), cols]
                mixed = headst[c][pl.ds(at_head, HD), at]
                delta = jnp.sum(grad.astype(F32) * mixed.astype(F32), axis=0, keepdims=True)
                grad = jnp.concatenate(
                    [grad, extra_rows(0.0, three_parts(-delta), tile).astype(BF)], 0
                )
                f = jnp.exp(dot(k[h], query, NN))
                g_scores = (f * dot(v[h], grad, NN)).astype(BF)
                f = f.astype(BF)
                g_query = dot(kt[h], g_scores, NN) * HD**-0.5
                g_query = turn(g_query, cos[:, cols], sin[:, cols], -1)
                gqkv[pl.ds(at_head, HD), cols] = g_query.astype(BF)
                more_v = dot(f, g[h, cols, :], NN)
                more_k = dot(g_scores, q[h, cols, :], NN)
                if c == 0 and n == 0:
                    dv[...] = more_v
                    dk[...] = more_k
                else:
                    dv[...] += more_v
                    dk[...] += more_k
        g_keys = turn(dk[...].T[:HD], cos[...], sin[...], -1)
        gqkv[pl.ds(pl.multiple_of((heads + h) * HD, HD), HD), :] = g_keys.astype(BF)
        g_values = dv[...].T
        gqkv[pl.ds(pl.multiple_of((2 * heads + h) * HD, HD), HD), :] = g_values.astype(BF)
        return 0

    lax.fori_loop(0, heads, one_head, 0)


def body(
    layer_input,
    lengths,
    w_qkv,
    w_out,
    w_gate,
    w_up,
    w_down,
    gain_one,
    bias_one,
    gain_two,
    bias_two,
    cotangent,
):
    _, piece, width = layer_input.shape
    local = w_qkv.shape[2]
    hidden_local = w_gate.shape[1]
    heads = local // HD
    seq = piece * TP
    half = seq // CHUNKS
    part = piece // CHUNKS
    me = lax.axis_index("tp")
    own = layer_input[0]
    cot = cotangent[0]
    wq = w_qkv.reshape(width, 3 * local)
    info = jnp.stack([lengths[0], (me * piece).astype(jnp.int32)])
    gain_one, bias_one, gain_two, bias_two = (
        a[None] for a in (gain_one, bias_one, gain_two, bias_two)
    )

    blocks = gather_blocks(own)
    block_of = jnp.bitwise_xor(me, jnp.arange(TP, dtype=jnp.int32)) * piece
    place = (
        jnp.arange(CHUNKS, dtype=jnp.int32)[:, None, None] * part
        + block_of[None, :, None]
        + jnp.arange(part, dtype=jnp.int32)[None, None, :]
    ).reshape(1, seq)
    frequency = 1000.0 ** (-jnp.arange(HD // 2, dtype=F32) * 2.0 / HD)
    angles = frequency[:, None] * place.astype(F32)
    cosine, sine = jnp.cos(angles), jnp.sin(angles)

    xg, qt, q, kt, k, vt, v = call(
        qkv_kernel,
        "qkv",
        [((seq, width), BF)]
        + [((heads, 2 * HD, seq), BF), ((heads, seq, 2 * HD), BF)]
        + [((heads, HD, seq), BF), ((heads, seq, 2 * HD), BF)]
        + [((heads, 2 * HD, seq), BF), ((heads, seq, 2 * HD), BF)],
        [info, *blocks, wq.T, cosine, sine, place],
        2 * seq * width * 3 * local,
        [pltpu.VMEM((3 * local, seq), F32)],
        smem=1,
    )

    def sums(rows):
        return [((2 * part, width), BF), ((part, width), F32), ((part, width), F32)]

    def cut(array, c):
        return array[c * part : (c + 1) * part]

    kept, firsts = [], []
    for c in range(CHUNKS):
        send, keep0, keep2, headst, lse = call(
            functools.partial(attend_kernel, c),
            f"attend_{c}",
            sums(part) + [((local, half), BF), ((heads, 1, half), F32)],
            [qt, k, vt, w_out],
            heads * seq * half * 512 + 2 * half * local * width,
        )
        got, back = scatter_blocks(send, keep2)
        kept.append((headst, lse))
        firsts.append(
            call(
                first_kernel,
                f"first_{c}",
                [((part, width), F32), ((part, 1), F32), ((part, width), BF)],
                [cut(own, c), keep0, got, back, gain_one, bias_one],
                part * width * 10,
            )
        )

    saved = []
    for c in range(CHUNKS):
        n1, r1, low = firsts[c]
        x, hidden, da, db, send, keep0, keep2 = call(
            ffn_kernel,
            f"ffn_{c}",
            [((half, width), BF)] + [((half, hidden_local), BF)] * 3 + sums(part),
            [*gather_blocks(low), w_gate, w_up, w_down],
            6 * half * width * hidden_local,
        )
        got, back = scatter_blocks(send, keep2)
        saved.append((x, hidden, da, db, keep0, got, back))

    seconds = []
    for c in range(CHUNKS):
        n1 = firsts[c][0]
        keep0, got, back = saved[c][4:]
        seconds.append(
            call(
                functools.partial(second_kernel, c),
                f"second_{c}",
                [((part, width), BF), ((part, width), F32), ((part, width), BF), ((2, width), F32)],
                [info, n1, gain_one, bias_one, keep0, got, back, gain_two, bias_two, cut(cot, c)],
                part * width * 30,
                smem=1,
            )
        )

    down_grad = pair_grad = 0.0
    lasts = []
    for c in range(CHUNKS):
        x, hidden, da, db = saved[c][:4]
        _, g_second, low, _ = seconds[c]
        n1, r1, _ = firsts[c]
        gf, gg, send, keep0, keep2 = call(
            ffn_back_kernel,
            f"ffn_back_{c}",
            [((half, width), BF), ((half, 2 * hidden_local), BF)] + sums(part),
            [*gather_blocks(low), w_gate, w_up, w_down, da, db],
            6 * half * width * hidden_local,
        )
        got, back = scatter_blocks(send, keep2)
        lasts.append(
            call(
                first_back_kernel,
                f"first_back_{c}",
                [((part, width), F32), ((part, width), BF), ((2, width), F32)],
                [g_second, keep0, got, back, n1, r1, gain_one],
                part * width * 20,
            )
        )
        down_grad = down_grad + dot(gf, hidden, TN)
        pair_grad = pair_grad + dot(x, gg, TN)
    small = jnp.concatenate([lasts[0][2] + lasts[1][2], seconds[0][3] + seconds[1][3]], 0)

    g_blocks = []
    for c in range(CHUNKS):
        g_blocks += gather_blocks(lasts[c][1])
    ga, gqkv = call(
        attend_back_kernel,
        "attend_back",
        [((seq, width), BF), ((3 * local, seq), BF)],
        [*g_blocks, w_out, qt, q, kt, k, v, cosine, sine]
        + [h for h, _ in kept]
        + [t for _, t in kept],
        heads * seq * seq * 1280 + 4 * seq * width * local,
        [
            pltpu.VMEM((local, seq), BF),
            pltpu.VMEM((heads, seq, HD), BF),
            pltpu.VMEM((seq, 2 * HD), F32),
            pltpu.VMEM((seq, HD), F32),
        ],
    )

    parts = dot(gqkv, wq, ((0,), (1,))).reshape(CHUNKS, TP, part, width)
    parts = [parts[:, j].reshape(piece, width) for j in range(TP)]
    got, back = scatter_blocks(
        jnp.concatenate([parts[1], parts[3]], 0).astype(BF), parts[2]
    )
    g_res = jnp.concatenate([last[0] for last in lasts], 0)
    input_grad = g_res + parts[0] + got[:piece].astype(F32) + back.astype(F32)

    qkv_grad = dot(xg, gqkv, ((0,), (1,)))
    headst = jnp.concatenate([h for h, _ in kept], 1)
    out_grad = dot(ga, headst, ((0,), (1,)))
    down_grad = scatter_dp(down_grad.astype(BF)).T
    pair_grad = scatter_dp(pair_grad.astype(BF))
    out_grad = scatter_dp(out_grad.astype(BF)).T
    qkv_grad = scatter_dp(qkv_grad.astype(BF))
    small = sum_all(small)
    return (
        jnp.concatenate([s[0] for s in seconds], 0)[None],
        input_grad[None],
        qkv_grad.reshape(-1, 3, local),
        out_grad,
        pair_grad[:, :hidden_local],
        pair_grad[:, hidden_local:],
        down_grad,
        small[0],
        small[1],
        small[2],
        small[3],
    )


def solution(mesh):
    placed = (
        P("dp", "tp", None),
        P("dp"),
        P(None, None, "tp"),
        P("tp", None),
        P(None, "tp"),
        P(None, "tp"),
        P("tp", None),
        P(),
        P(),
        P(),
        P(),
        P("dp", "tp", None),
    )
    return jax.shard_map(
        body,
        mesh=mesh,
        in_specs=placed,
        out_specs=(
            P("dp", "tp", None),
            P("dp", "tp", None),
            P("dp", None, "tp"),
            P("tp", "dp"),
            P("dp", "tp"),
            P("dp", "tp"),
            P("tp", "dp"),
            P(),
            P(),
            P(),
            P(),
        ),
        check_vma=False,
    )
```

```python
import functools

import jax
import jax.numpy as jnp
from jax import lax
from jax.experimental import pallas as pl
from jax.experimental.pallas import tpu as pltpu
from jax.sharding import PartitionSpec as P

HD = 64
CHUNKS = 2
TP = 4

masked_score = -1e30
epsilon = 1e-05


BF = jnp.bfloat16
F32 = jnp.float32
NN = ((1,), (0,))
NT = ((1,), (1,))
TN = ((0,), (0,))


def dot(a, b, dims):
    return lax.dot_general(a, b, (dims, ((), ())), preferred_element_type=F32)


def swap(values, axis, mask):
    size = lax.axis_size(axis)
    return lax.ppermute(values, axis, [(i, i ^ mask) for i in range(size)])


def gather_blocks(block):
    across = swap(block, "tp", 2)
    beside = swap(block, "tp", 1)
    return [block, beside, across, swap(across, "tp", 1)]


def scatter_near(send, keep_away):
    rows = send.shape[0] // 2
    got = swap(send, "tp", 1)
    return got, (keep_away + got[rows:].astype(F32)).astype(BF)


def scatter_blocks(send, keep_away):
    got, away = scatter_near(send, keep_away)
    return got, swap(away, "tp", 2)


def after(value, *deps):
    return lax.optimization_barrier((value, *deps))[0]


def deal(total, send, keep, bit, rows, pairs):
    for m in range(pairs):
        at = slice(m * rows, (m + 1) * rows)
        theirs = pl.multiple_of((2 * m + 1 - bit) * rows, rows)
        ours = pl.multiple_of((2 * m + bit) * rows, rows)
        send[at, :] = total[pl.ds(theirs, rows), :].astype(BF)
        keep[at, :] = total[pl.ds(ours, rows), :].astype(BF)


def deal_kernel(rows, pairs, info, grad, send, keep, total):
    total[...] = grad[...].astype(F32)
    deal(total, send, keep, info[2] % 2, rows, pairs)


def small_parts(total):
    hi = total.astype(BF).astype(F32)
    return jnp.concatenate([hi, total - hi], 0)


def merge_kernel(step, rows, pairs, extra, info, keep, got, send, kept, total):
    size = 2 * pairs * rows
    summed = keep[...].astype(F32) + got[...].astype(F32)
    total[...] = summed[:size]
    deal(total, send, kept, (info[2] // step) % 2, rows, pairs)
    if extra:
        small = []
        for at in (size, size + 8):
            small.append(small_parts(summed[at : at + 4] + summed[at + 4 : at + 8]))
        small = jnp.concatenate(small, 0).astype(BF)
        send[pairs * rows :, :] = small
        kept[pairs * rows :, :] = small


def dealt_shapes(size, rows, cols, extra=0):
    return [((size // 2 * rows + extra, cols), BF)] * 2


def start_dp(info, grad, size):
    rows, cols = grad.shape[0] // size, grad.shape[1]
    return call(
        functools.partial(deal_kernel, rows, size // 2),
        "deal",
        dealt_shapes(size, rows, cols),
        [info, grad],
        grad.size,
        [pltpu.VMEM(grad.shape, F32)],
        smem=1,
    )


def scatter_dp(info, send, keep, size, extra=0):
    step, left = 1, size // 2
    rows = (keep.shape[0] - extra) // left
    cols = keep.shape[1]
    while True:
        got = swap(send, "dp", step)
        if left == 1:
            return keep, got
        step *= 2
        send, keep = call(
            functools.partial(merge_kernel, step, rows, left // 2, extra),
            f"merge_{step}",
            dealt_shapes(left, rows, cols, extra),
            [info, keep, got],
            keep.size,
            [pltpu.VMEM((left * rows, cols), F32)],
            smem=1,
        )
        left //= 2


def plain_scatter_dp(grad, size):
    me = lax.axis_index("dp")
    cols = grad.shape[1]
    rows = grad.shape[0] // size
    step = 1
    while step < size:
        bit = (me // step) % 2
        view = grad.reshape(size // step // 2, 2, rows, cols)
        send = lax.dynamic_index_in_dim(view, 1 - bit, 1, keepdims=False).astype(BF)
        keep = lax.dynamic_index_in_dim(view, bit, 1, keepdims=False)
        grad = keep.astype(F32) + swap(send, "dp", step).astype(F32)
        step *= 2
        if step < size:
            grad = grad.astype(BF)
    return grad.reshape(rows, cols)


def pair_end_kernel(keep, got, gate, up):
    total = keep[...].astype(F32) + got[...].astype(F32)
    half = total.shape[1] // 2
    gate[...] = total[:, :half]
    up[...] = total[:, half:]


def down_end_kernel(keep, got, down):
    down[...] = keep[...].astype(F32) + got[...].astype(F32)


def most_end_kernel(keep, got, grad, out, small0, small1):
    rows, wide = grad.shape
    total = keep[...].astype(F32) + got[...].astype(F32)
    grad[...] = total[:rows, :wide]
    out[...] = total[:rows, wide:]
    small0[...] = total[rows : rows + 4] + total[rows + 4 : rows + 8]
    small1[...] = total[rows + 8 : rows + 12] + total[rows + 12 : rows + 16]


def last_end_kernel(places, most, keep, got, grad):
    rows = most.shape[0]
    last = keep[:rows].astype(F32) + got[:rows].astype(F32)
    for at, (group, start) in enumerate(places):
        source = (most[...], last)[group]
        grad[:, at * HD : (at + 1) * HD] = source[:, start : start + HD]


def order_of(heads):
    place, names = {}, []
    for group, members in enumerate((range(heads - 1), range(heads - 1, heads))):
        start = 0
        for what in [(c, h) for h in members for c in (0, 1)] + [(2, h) for h in members]:
            place[what] = (group, start)
            names.append(what)
            start += HD
    return place, names


def sum_dp(values):
    step = 1
    while step < lax.axis_size("dp"):
        values = values + swap(values, "dp", step)
        step *= 2
    return values


def call(kernel, name, outs, args, flops, scratch=(), smem=0, limit=12):
    specs = [pl.BlockSpec(memory_space=pltpu.SMEM)] * smem
    specs += [pl.BlockSpec(memory_space=pltpu.VMEM)] * (len(args) - smem)
    shapes = [jax.ShapeDtypeStruct(s, d) for s, d in outs]
    moved = sum(a.size * a.dtype.itemsize for a in args)
    moved += sum(s.size * s.dtype.itemsize for s in shapes)
    return pl.pallas_call(
        kernel,
        name=name,
        out_shape=shapes,
        in_specs=specs,
        out_specs=[pl.BlockSpec(memory_space=pltpu.VMEM)] * len(shapes),
        scratch_shapes=list(scratch),
        compiler_params=pltpu.CompilerParams(vmem_limit_bytes=limit * 1024 * 1024),
        cost_estimate=pl.CostEstimate(flops=flops, bytes_accessed=moved, transcendentals=0),
    )(*args)


def turn(values, cosine, sine, direction):
    half = values.shape[0] // 2
    lower, upper = values[:half], values[half:]
    if direction > 0:
        return jnp.concatenate([lower * cosine - upper * sine, upper * cosine + lower * sine], 0)
    return jnp.concatenate([lower * cosine + upper * sine, upper * cosine - lower * sine], 0)


def three_parts(row):
    hi = row.astype(BF).astype(F32)
    rest = row - hi
    mid = rest.astype(BF).astype(F32)
    return hi, mid, rest - mid


def extra_rows(first, parts, count):
    row = lax.broadcasted_iota(jnp.int32, (64, count), 0)
    out = jnp.where(row == 0, first, 0.0)
    for k, part in enumerate(parts):
        out = jnp.where(row == k + 1, part, out)
    return out


def qkv_kernel(info, b0, b1, b2, b3, wt, cos, sin, pos, xg, qt, q, kt, k, vt, v, full):
    blocks = (b0, b1, b2, b3)
    piece = b0.shape[0]
    part = piece // CHUNKS
    heads = wt.shape[0] // (3 * HD)
    for j in range(TP):
        for c in range(CHUNKS):
            at = (c * TP + j) * part
            xg[at : at + part, :] = blocks[j][c * part : (c + 1) * part, :]
    seq = piece * TP
    half = seq // CHUNKS
    for c in range(CHUNKS):
        cols = slice(c * half, (c + 1) * half)
        full[:, cols] = dot(wt[...], xg[cols, :], NT)
    place, names = order_of(heads)

    def offset(c, h):
        return names.index((c, h)) * HD

    ones = (1.0, 1.0, 1.0)
    bias = jnp.where(pos[...] < info[0], 0.0, masked_score)
    for c in range(CHUNKS):
        cols = slice(c * half, (c + 1) * half)
        cosine, sine = cos[:, cols], sin[:, cols]
        for h in range(heads):
            at = offset(0, h)
            query = turn(full[at : at + HD, cols], cosine, sine, 1) * HD**-0.5
            query = jnp.concatenate([query, extra_rows(1.0, (0.0, 0.0, 0.0), half)], 0)
            qt[h, :, cols] = query.astype(BF)
            q[h, cols, :] = query.T.astype(BF)
            at = offset(1, h)
            keys = turn(full[at : at + HD, cols], cosine, sine, 1)
            keys = jnp.concatenate([keys, extra_rows(bias[:, cols], ones, half)], 0)
            kt[h, :, cols] = keys[:HD].astype(BF)
            k[h, cols, :] = keys.T.astype(BF)
            at = offset(2, h)
            values = jnp.concatenate([full[at : at + HD, cols], extra_rows(0.0, ones, half)], 0)
            vt[h, :, cols] = values.astype(BF)
            v[h, cols, :] = values.T.astype(BF)


def attend_kernel(chunk, qt, k, vt, wo, send, keep0, keep2, headst, lse):
    heads = qt.shape[0]
    count = headst.shape[1]
    part = count // TP
    tile = 256
    tiles = count // tile

    def step(i, _):
        h, at = i // tiles, pl.multiple_of((i % tiles) * tile, tile)
        query = qt[h, :, pl.ds(chunk * count + at, tile)]
        scores = dot(k[h], query, NN)
        top = jnp.max(scores, axis=0, keepdims=True)
        exps = jnp.exp(scores - top).astype(BF)
        mixed = dot(vt[h, :80, :], exps, NN)
        total = mixed[HD + 1 : HD + 2]
        mixed = (mixed[:HD] / total).astype(BF)
        headst[pl.ds(pl.multiple_of(h * HD, HD), HD), pl.ds(at, tile)] = mixed
        lse[h, :, pl.ds(at, tile)] = top + jnp.log(total)
        return 0

    lax.fori_loop(0, heads * tiles, step, 0)
    mixed = headst[...].T
    out = dot(mixed, wo[...], NN)
    keep0[...] = out[:part]
    send[:part, :] = out[part : 2 * part].astype(BF)
    keep2[...] = out[2 * part : 3 * part]
    send[part:, :] = out[3 * part :].astype(BF)


def norm(values):
    center = values - jnp.mean(values, axis=-1, keepdims=True)
    inverse = lax.rsqrt(jnp.mean(center * center, axis=-1, keepdims=True) + epsilon)
    return center * inverse, inverse


def norm_grad(upstream, normed, inverse, gain):
    scaled = upstream * gain
    return inverse * (
        scaled
        - jnp.mean(scaled, axis=-1, keepdims=True)
        - normed * jnp.mean(scaled * normed, axis=-1, keepdims=True)
    )


def first_kernel(x, keep0, got, back, gain, bias, n1, r1, low):
    part = x.shape[0]
    summed = x[...].astype(F32) + keep0[...] + got[:part].astype(F32) + back[...].astype(F32)
    normed, inverse = norm(summed)
    n1[...] = normed
    r1[...] = inverse
    low[...] = (normed * gain[...] + bias[...]).astype(BF)


def ffn_kernel(b0, b1, b2, b3, wg, wu, wd, x, hidden, da, db, send, keep0, keep2):
    part, width = b0.shape
    for j, block in enumerate((b0, b1, b2, b3)):
        x[j * part : (j + 1) * part, :] = block[...]
    tile = 256
    for n in range(wg.shape[1] // tile):
        cols = slice(n * tile, (n + 1) * tile)
        gate = dot(x[...], wg[:, cols], NN)
        up = dot(x[...], wu[:, cols], NN)
        sg = jax.nn.sigmoid(gate)
        act = gate * sg
        hidden[:, cols] = (act * up).astype(BF)
        da[:, cols] = (up * sg * (1.0 + gate * (1.0 - sg))).astype(BF)
        db[:, cols] = act.astype(BF)
    for n in range(width // tile):
        cols = slice(n * tile, (n + 1) * tile)
        out = dot(hidden[...], wd[:, cols], NN)
        keep0[:, cols] = out[:part]
        send[:part, cols] = out[part : 2 * part].astype(BF)
        keep2[:, cols] = out[2 * part : 3 * part]
        send[part:, cols] = out[3 * part :].astype(BF)


def second_kernel(
    chunk, info, n1, gain_one, bias_one, keep0, got, back, gain, bias, cot, out, gsec, glow, small
):
    part = n1.shape[0]
    first = n1[...] * gain_one[...] + bias_one[...]
    ffn = keep0[...] + got[:part].astype(F32) + back[...].astype(F32)
    n2, r2 = norm(first + ffn)
    row = info[1] + chunk * part + lax.broadcasted_iota(jnp.int32, (part, 1), 0)
    valid = jnp.where(row < info[0], 1.0, 0.0)
    out[...] = (valid * (n2 * gain[...] + bias[...])).astype(BF)
    g_out = cot[...].astype(F32) * valid
    g_second = norm_grad(g_out, n2, r2, gain[...])
    gsec[...] = g_second
    glow[...] = g_second.astype(BF)
    small[0:1, :] = jnp.sum(g_out * n2, axis=0, keepdims=True)
    small[1:2, :] = jnp.sum(g_out, axis=0, keepdims=True)


def ffn_back_kernel(b0, b1, b2, b3, wg, wu, wd, da, db, gf, gg, send, keep0, keep2):
    part, width = b0.shape
    for j, block in enumerate((b0, b1, b2, b3)):
        gf[j * part : (j + 1) * part, :] = block[...]
    tile = 256
    hidden = wg.shape[1]
    for n in range(hidden // tile):
        cols = slice(n * tile, (n + 1) * tile)
        more = slice(hidden + n * tile, hidden + (n + 1) * tile)
        g_hidden = dot(gf[...], wd[cols, :], NT)
        gg[:, cols] = (g_hidden * da[:, cols].astype(F32)).astype(BF)
        gg[:, more] = (g_hidden * db[:, cols].astype(F32)).astype(BF)
    for n in range(width // tile):
        cols = slice(n * tile, (n + 1) * tile)
        out = dot(gg[:, :hidden], wg[cols, :], NT) + dot(gg[:, hidden:], wu[cols, :], NT)
        keep0[:, cols] = out[:part]
        send[:part, cols] = out[part : 2 * part].astype(BF)
        keep2[:, cols] = out[2 * part : 3 * part]
        send[part:, cols] = out[3 * part :].astype(BF)


def first_back_kernel(gsec, keep0, got, back, n1, r1, gain, second, gres, low):
    part = n1.shape[0]
    g_first = gsec[...] + keep0[...] + got[:part].astype(F32) + back[...].astype(F32)
    normed = n1[...]
    g_res = norm_grad(g_first, normed, r1[...], gain[...])
    gres[...] = g_res
    low[:part, :] = g_res.astype(BF)
    one = [jnp.sum(g_first * normed, axis=0, keepdims=True)]
    one += [jnp.sum(g_first, axis=0, keepdims=True), second[...]]
    rows = small_parts(jnp.concatenate(one, 0))
    low[part:, :] = jnp.concatenate([rows, jnp.zeros_like(rows)], 0).astype(BF)


def prepare_kernel(*refs):
    blocks = refs[: TP * CHUNKS]
    wo, ga, gt, g, small = refs[TP * CHUNKS :]
    heads = g.shape[0]
    half = ga.shape[0] // CHUNKS
    part = half // TP
    total = 0.0
    for b, block in enumerate(blocks):
        ga[b * part : (b + 1) * part, :] = block[:part, :]
        rows = block[part:, :].astype(F32)
        total = total + rows[:4] + rows[4:8]
    small[...] = total
    for c in range(CHUNKS):
        rows = slice(c * half, (c + 1) * half)
        gt[:, rows] = dot(wo[...], ga[rows, :], NT).astype(BF)
        for h in range(heads):
            g[h, rows, :] = dot(ga[rows, :], wo[h * HD : (h + 1) * HD, :], NT).astype(BF)


def attend_back_kernel(members, size, split, wide, *refs):
    info, qt, q, kt, k, v, gt, g, cos, sin, xt = refs[:11]
    rest = refs[11:]
    headst, lse = rest[:CHUNKS], rest[CHUNKS : 2 * CHUNKS]
    rest = rest[2 * CHUNKS :]
    if wide:
        out_grad, small = rest[:2]
        rest = rest[2:]
    if split:
        gq, send, keep, dq, dk, dv, total = rest
    else:
        gq, whole, dq, dk, dv, total = rest
    seq = gq.shape[0]
    half = seq // CHUNKS
    tile = 256

    def one_head(i, _):
        h = members.start + i
        at_head = pl.multiple_of(h * HD, HD)
        for c in range(CHUNKS):
            for n in range(half // tile):
                at = slice(n * tile, (n + 1) * tile)
                cols = slice(c * half + n * tile, c * half + (n + 1) * tile)
                top = lse[c][h, :, at]
                query = jnp.concatenate(
                    [
                        qt[h, :HD, cols],
                        extra_rows(1.0, three_parts(-top), tile).astype(BF),
                    ],
                    0,
                )
                grad = gt[pl.ds(at_head, HD), cols]
                mixed = headst[c][pl.ds(at_head, HD), at]
                delta = jnp.sum(grad.astype(F32) * mixed.astype(F32), axis=0, keepdims=True)
                grad = jnp.concatenate(
                    [grad, extra_rows(0.0, three_parts(-delta), tile).astype(BF)], 0
                )
                f = jnp.exp(dot(k[h], query, NN))
                g_scores = (f * dot(v[h], grad, NN)).astype(BF)
                f = f.astype(BF)
                g_query = dot(kt[h], g_scores, NN) * HD**-0.5
                dq[i, :, cols] = turn(g_query, cos[:, cols], sin[:, cols], -1)
                more_v = dot(f, g[h, cols, :], NN)
                more_k = dot(g_scores, q[h, cols, :], NN)
                if c == 0 and n == 0:
                    dv[i] = more_v
                    dk[i] = more_k
                else:
                    dv[i] += more_v
                    dk[i] += more_k
        return 0

    count = len(members)
    lax.fori_loop(0, count, one_head, 0)
    for i in range(count):
        g_keys = turn(dk[i].T[:HD], cos[...], sin[...], -1)
        both = jnp.concatenate([dq[i], g_keys], 0)
        gq[:, 2 * i * HD : 2 * (i + 1) * HD] = both.T.astype(BF)
    at = 2 * count * HD
    gq[:, at : at + count * HD] = jnp.concatenate([dv[i] for i in range(count)], 1).astype(BF)
    cols = gq.shape[1]
    total[:, :cols] = dot(xt[...], gq[...], NN)
    if wide:
        total[:, cols:] = out_grad[...]
    if not split:
        whole[...] = total[...].astype(BF)
        return
    rows = total.shape[0] // size
    deal(total, send, keep, info[2] % 2, rows, size // 2)
    if wide:
        parts = small_parts(small[...])
        across = total.shape[1]
        rest = parts[:, across:]
        pad = jnp.zeros((8, across - rest.shape[1]), F32)
        parts = jnp.concatenate([parts[:, :across], jnp.concatenate([rest, pad], 1)], 0)
        send[size // 2 * rows :, :] = parts.astype(BF)
        keep[size // 2 * rows :, :] = parts.astype(BF)


def input_kernel(gq0, gq1, wt, send, keep0, keep2):
    seq, wide = gq0.shape
    width = wt.shape[1]
    half = seq // CHUNKS
    part = half // TP
    piece = part * CHUNKS
    for c in range(CHUNKS):
        rows = slice(c * half, (c + 1) * half)
        out = dot(gq0[rows, :], wt[:wide, :], NN) + dot(gq1[rows, :], wt[wide:, :], NN)
        at = slice(c * part, (c + 1) * part)
        away = slice(piece + c * part, piece + (c + 1) * part)
        keep0[at, :] = out[:part]
        send[at, :] = out[part : 2 * part].astype(BF)
        keep2[at, :] = out[2 * part : 3 * part]
        send[away, :] = out[3 * part :].astype(BF)


def body(
    layer_input,
    lengths,
    w_qkv,
    w_out,
    w_gate,
    w_up,
    w_down,
    gain_one,
    bias_one,
    gain_two,
    bias_two,
    cotangent,
):
    _, piece, width = layer_input.shape
    local = w_qkv.shape[2]
    hidden_local = w_gate.shape[1]
    heads = local // HD
    seq = piece * TP
    half = seq // CHUNKS
    part = piece // CHUNKS
    me = lax.axis_index("tp")
    own = layer_input[0]
    cot = cotangent[0]
    place_of, names = order_of(heads)
    wt = w_qkv.reshape(width, 3 * heads, HD)
    wt = jnp.concatenate([wt[:, c * heads + h] for c, h in names], 1).T
    dp = lax.axis_size("dp")
    split = (width // dp) % 16 == 0
    info = jnp.stack([lengths[0], me * piece, lax.axis_index("dp")]).astype(jnp.int32)
    gain_one, bias_one, gain_two, bias_two = (
        a[None] for a in (gain_one, bias_one, gain_two, bias_two)
    )

    blocks = gather_blocks(own)
    block_of = jnp.bitwise_xor(me, jnp.arange(TP, dtype=jnp.int32)) * piece
    place = (
        jnp.arange(CHUNKS, dtype=jnp.int32)[:, None, None] * part
        + block_of[None, :, None]
        + jnp.arange(part, dtype=jnp.int32)[None, None, :]
    ).reshape(1, seq)
    frequency = 1000.0 ** (-jnp.arange(HD // 2, dtype=F32) * 2.0 / HD)
    angles = frequency[:, None] * place.astype(F32)
    cosine, sine = jnp.cos(angles), jnp.sin(angles)

    xg, qt, q, kt, k, vt, v = call(
        qkv_kernel,
        "qkv",
        [((seq, width), BF)]
        + [((heads, 2 * HD, seq), BF), ((heads, seq, 2 * HD), BF)]
        + [((heads, HD, seq), BF), ((heads, seq, 2 * HD), BF)]
        + [((heads, 2 * HD, seq), BF), ((heads, seq, 2 * HD), BF)],
        [info, *blocks, wt, cosine, sine, place],
        2 * seq * width * 3 * local,
        [pltpu.VMEM((3 * local, seq), F32)],
        smem=1,
    )

    def sums(rows):
        return [((2 * part, width), BF), ((part, width), F32), ((part, width), F32)]

    def cut(array, c):
        return array[c * part : (c + 1) * part]

    xt = xg.T
    kept, firsts = [], []
    for c in range(CHUNKS):
        send, keep0, keep2, headst, lse = call(
            functools.partial(attend_kernel, c),
            f"attend_{c}",
            sums(part) + [((local, half), BF), ((heads, 1, half), F32)],
            [qt, k, vt, w_out],
            heads * seq * half * 512 + 2 * half * local * width,
        )
        got, away = scatter_near(send, keep2)
        if c + 1 < CHUNKS:
            qt, away = lax.optimization_barrier((qt, away))
        back = swap(away, "tp", 2)
        kept.append((headst, lse))
        firsts.append(
            call(
                first_kernel,
                f"first_{c}",
                [((part, width), F32), ((part, 1), F32), ((part, width), BF)],
                [cut(own, c), keep0, got, back, gain_one, bias_one],
                part * width * 10,
            )
        )

    saved = []
    for c in range(CHUNKS):
        n1, r1, low = firsts[c]
        x, hidden, da, db, send, keep0, keep2 = call(
            ffn_kernel,
            f"ffn_{c}",
            [((half, width), BF)] + [((half, hidden_local), BF)] * 3 + sums(part),
            [*gather_blocks(low), w_gate, w_up, w_down],
            6 * half * width * hidden_local,
        )
        got, back = scatter_blocks(send, keep2)
        saved.append((x, hidden, da, db, keep0, got, back))

    seconds = []
    for c in range(CHUNKS):
        n1 = firsts[c][0]
        keep0, got, back = saved[c][4:]
        seconds.append(
            call(
                functools.partial(second_kernel, c),
                f"second_{c}",
                [((part, width), BF), ((part, width), F32), ((part, width), BF), ((2, width), F32)],
                [info, n1, gain_one, bias_one, keep0, got, back, gain_two, bias_two, cut(cot, c)],
                part * width * 30,
                smem=1,
            )
        )

    down_grad = pair_grad = 0.0
    lasts = []
    for c in range(CHUNKS):
        x, hidden, da, db = saved[c][:4]
        _, g_second, low, _ = seconds[c]
        n1, r1, _ = firsts[c]
        gf, gg, send, keep0, keep2 = call(
            ffn_back_kernel,
            f"ffn_back_{c}",
            [((half, width), BF), ((half, 2 * hidden_local), BF)] + sums(part),
            [*gather_blocks(low), w_gate, w_up, w_down, da, db],
            6 * half * width * hidden_local,
        )
        got, back = scatter_blocks(send, keep2)
        lasts.append(
            call(
                first_back_kernel,
                f"first_back_{c}",
                [((part, width), F32), ((part + 16, width), BF)],
                [g_second, keep0, got, back, n1, r1, gain_one, seconds[c][3]],
                part * width * 20,
            )
        )
        down_grad = down_grad + dot(gf, hidden, TN)
        pair_grad = pair_grad + dot(x, gg, TN)
    down_grad, pair_grad = down_grad.astype(BF), pair_grad.astype(BF)
    if split:
        down_grad = scatter_dp(info, *start_dp(info, down_grad, dp), dp)
        pair_grad = scatter_dp(info, *start_dp(info, pair_grad, dp), dp)

    g_blocks = []
    for c in range(CHUNKS):
        g_blocks += gather_blocks(lasts[c][1])
    ga, gt, g, small = call(
        prepare_kernel,
        "prepare",
        [((seq, width), BF), ((local, seq), BF), ((heads, seq, HD), BF), ((4, width), F32)],
        [*g_blocks, w_out],
        4 * seq * width * local,
    )
    headst = jnp.concatenate([h for h, _ in kept], 1)
    out_grad = dot(ga, headst, ((0,), (1,)))

    gqs, grads = [], []
    for wide, members in ((True, range(heads - 1)), (False, range(heads - 1, heads))):
        count = len(members)
        cols = 3 * HD * count
        across = cols + (local if wide else 0)
        shape = [((width, across), BF)]
        if split:
            shape = dealt_shapes(dp, width // dp, across, 16 if wide else 0)
        gq, *grad = call(
            functools.partial(attend_back_kernel, members, dp, split, wide),
            "attend_back",
            [((seq, cols), BF)] + shape,
            [info, qt, q, kt, k, v, gt, g, cosine, sine, xt]
            + [h for h, _ in kept]
            + [t for _, t in kept]
            + ([out_grad, small] if wide else []),
            count * seq * seq * 1280 + 2 * seq * width * cols,
            [
                pltpu.VMEM((count, HD, seq), F32),
                pltpu.VMEM((count, seq, 2 * HD), F32),
                pltpu.VMEM((count, seq, HD), F32),
                pltpu.VMEM((width, across), F32),
            ],
            smem=1,
            limit=20,
        )
        gqs.append(gq)
        if split:
            grads.append(scatter_dp(info, *grad, dp, 16 if wide else 0))
        else:
            grads.append(grad[0])

    send, keep0, keep2 = call(
        input_kernel,
        "input",
        [((2 * piece, width), BF), ((piece, width), F32), ((piece, width), F32)],
        [*gqs, wt],
        2 * seq * width * 3 * local,
    )
    got, back = scatter_blocks(send, keep2)
    g_res = jnp.concatenate([last[0] for last in lasts], 0)
    input_grad = g_res + keep0 + got[:piece].astype(F32) + back.astype(F32)

    cols = 3 * HD * (heads - 1)
    if split:
        rows = width // dp
        (down_grad,) = call(
            down_end_kernel, "down_end", [((rows, width), F32)], down_grad, rows * width
        )
        gate_grad, up_grad = call(
            pair_end_kernel,
            "pair_end",
            [((rows, hidden_local), F32)] * 2,
            pair_grad,
            rows * width,
        )
        across = cols + local
        most, out_grad, small0, small1 = call(
            most_end_kernel,
            "most_end",
            [((rows, cols), F32), ((rows, local), F32), ((4, across), F32), ((4, across), F32)],
            grads[0],
            rows * across,
        )
        small = jnp.concatenate([small0, small1[:, : width - across]], 1)
        places = [place_of[c, h] for c in range(3) for h in range(heads)]
        (qkv_grad,) = call(
            functools.partial(last_end_kernel, places),
            "last_end",
            [((rows, 3 * local), F32)],
            [most, *grads[1]],
            rows * 3 * local,
        )
    else:
        down_grad = plain_scatter_dp(down_grad, dp)
        pair_grad = plain_scatter_dp(pair_grad, dp)
        gate_grad, up_grad = pair_grad[:, :hidden_local], pair_grad[:, hidden_local:]
        most, last = (plain_scatter_dp(a, dp) for a in grads)
        most, out_grad = most[:, :cols], most[:, cols:]
        places = [place_of[c, h] for c in range(3) for h in range(heads)]
        qkv_grad = jnp.concatenate([(most, last)[g][:, s : s + HD] for g, s in places], 1)
        small = sum_dp(small)
    return (
        jnp.concatenate([s[0] for s in seconds], 0)[None],
        input_grad[None],
        qkv_grad.reshape(-1, 3, local),
        out_grad.T,
        gate_grad,
        up_grad,
        down_grad.T,
        small[0],
        small[1],
        small[2],
        small[3],
    )


def solution(mesh):
    placed = (
        P("dp", "tp", None),
        P("dp"),
        P(None, None, "tp"),
        P("tp", None),
        P(None, "tp"),
        P(None, "tp"),
        P("tp", None),
        P(),
        P(),
        P(),
        P(),
        P("dp", "tp", None),
    )
    return jax.shard_map(
        body,
        mesh=mesh,
        in_specs=placed,
        out_specs=(
            P("dp", "tp", None),
            P("dp", "tp", None),
            P("dp", None, "tp"),
            P("tp", "dp"),
            P("dp", "tp"),
            P("dp", "tp"),
            P("tp", "dp"),
            P(),
            P(),
            P(),
            P(),
        ),
        check_vma=False,
    )
```
